32 devices in a mesh: ga: 8 (over z, x), band: 2 (over y), pool: 2 (over core).
Axes of the slice: x: 2, y: 2, z: 4, core: 2. Of those that a mesh axis runs over, the one named last changes fastest.
Arguments:
- psi_occ: bfloat16 [512, 64, 64, 128], P(('pool', 'band'), 'ga'), parts along dimension 0, may hold values from -9 to 9
- energies: float32 [32], P(('pool', 'band')), parts along dimension 0, may hold values from -0.8 to 0.6
- k_point: float32 [6], P('pool'), parts along dimension 0, may hold values from -0.5 to 0.5, as said below
- g_mask: int32 [128, 4096], P(('pool', 'ga')), parts along dimension 0, may hold values from 0 to 1, as said below
- v_local: float32 [64, 4096], P(None, 'ga'), may hold values from 1 to 4
- dv: float32 [3, 64, 4096], P(None, None, 'ga'), may hold values from -6 to 6
Outputs:
- response: float32 [32, 3, 64, 64, 128], P(('pool', 'band'), None, 'ga'), parts along dimension 0
- residual: float32 [32, 3, 64, 64, 128], P(('pool', 'band'), None, 'ga'), parts along dimension 0
The draws below stay inside these ranges and needn't reach their ends.
There are 2 independent parts, one for each index of `pool`. The reference program is written for one: setup_inputs(seed, part) draws one part's arguments, and reference() takes and returns one part's arrays. A program takes and returns all parts, laid end to end along the dimension named above; an argument that names none is the same for every part. Nothing has to cross between parts.
Inputs may be any that keep to these rules, and one draw needn't show every extreme that they name: `k_point`: each component is a nonzero multiple of 0.25. `g_mask`: 1 exactly where the distance of (f(g1), f(g2), f(g3)) + k_point from the anchor is below 21, with f the signed frequency; so no 1 stands where |f(g2)| > 21 or |f(g3)| > 21, and in every draw some 1 stands where |f(g2)| = 21.
All inputs are finite; a program needn't handle non-finite values.
Results may differ from the reference program's by a relative error of at most 0.0044.
Values may be sent and summed in bfloat16 or wider, within the bound.
No kernel may reach another device: no remote copies, remote signals or barrier semaphores. Data moves between devices by JAX's collectives and lax.ppermute only.
A program may use at most 192 MiB of HBM per device.

```python
import math
import jax
import jax.numpy as jnp
from jax import lax

BOX = 64
GCUT = 21
NOCC = 256
NSOLVE = 16
NPERT = 3
ITERS = 2
STRIDE = 16


def offset_steps(key):
    picks = jax.random.randint(jax.random.fold_in(key, 11), (3,), 0, 4)
    return jnp.where(picks < 2, picks - 2, picks - 1).astype(jnp.int32)


def draw_k_point(key, part):
    return offset_steps(key).astype(jnp.float32) * 0.25


def draw_g_mask(key, part):
    shifts = offset_steps(key)
    indices = jnp.arange(BOX, dtype=jnp.int32)
    signed = jnp.where(indices < BOX // 2, indices, indices - BOX)
    first = 4 * signed[:, None, None] + shifts[0]
    second = 4 * signed[None, :, None] + shifts[1]
    third = 4 * signed[None, None, :] + shifts[2]
    total = first * first + second * second + third * third
    inside = (total < 16 * GCUT * GCUT).astype(jnp.int32)
    return inside.reshape(BOX, BOX * BOX)


def shard_levels(rng, extent, split, smallest, largest):
    gain, own = 1.0, jax.random.fold_in(rng, 6)
    for position, blocks in split:
        steps = jnp.exp(jax.random.uniform(jax.random.fold_in(own, position), (blocks,), jnp.float32, smallest / len(split), largest / len(split)))
        gain = gain * jnp.repeat(steps, extent[position] // blocks).reshape([-1 if axis == position else 1 for axis in range(len(extent))])
    return gain


def centred(stream_key, shape, scale, most, pieces=(), held_as=jnp.bfloat16):
    factor_of = shard_levels(stream_key, shape, pieces, -0.22, 0.18) if pieces else 1.0
    array = jax.random.normal(stream_key, shape, jnp.float32) * scale * factor_of
    return jnp.minimum(jnp.maximum(array, -most), most).astype(held_as)


def setup_inputs(seed: int = 0, part: int = 0) -> dict:
    splits = jax.random.split(jax.random.key(seed), 7)
    part_keys = jax.random.split(jax.random.fold_in(splits[6], part), 7)
    psi_occ = centred(part_keys[0], (NOCC, BOX, BOX, 2 * BOX), 1.8, 9.0, ((0, 2), (1, 8)))
    energies = jnp.clip(-0.8 + 1.40000004 * jax.random.uniform(part_keys[1], (NSOLVE,), jnp.float32) ** shard_levels(part_keys[1], (NSOLVE,), ((0, 2),), -0.2, 0.2), -0.8, 0.6)
    k_point = draw_k_point(jax.random.fold_in(jax.random.fold_in(splits[6], part), 71), part)
    g_mask = draw_g_mask(jax.random.fold_in(jax.random.fold_in(splits[6], part), 71), part)
    v_local = jnp.clip(1.0 + 3.0 * jax.random.uniform(splits[4], (BOX, BOX * BOX), jnp.float32) ** shard_levels(splits[4], (BOX, BOX * BOX), ((1, 8),), -0.2, 0.2), 1.0, 4.0)
    dv = centred(splits[5], (NPERT, BOX, BOX * BOX), 1.0, 6.0, ((2, 8),), jnp.float32)
    return dict(psi_occ=psi_occ, energies=energies, k_point=k_point, g_mask=g_mask, v_local=v_local, dv=dv)


cell_length = 16.5
shift_weight = 8.0


def rounded(values):
    return lax.optimization_barrier(values.astype(jnp.bfloat16)).astype(jnp.float32)


def complex_form(halves):
    return halves[..., :BOX] + 1j * halves[..., BOX:]


def signed_freq():
    indices = jnp.arange(BOX, dtype=jnp.int32)
    return jnp.where(indices < BOX // 2, indices, indices - BOX).astype(jnp.float32)


def kept_indices():
    return jnp.concatenate([jnp.arange(GCUT + 1, dtype=jnp.int32), jnp.arange(BOX - GCUT, BOX, dtype=jnp.int32)]).astype(jnp.int32)


def cube_of(values):
    keep = kept_indices()
    values = jnp.take(values, keep, axis=values.ndim - 3)
    values = jnp.take(values, keep, axis=values.ndim - 2)
    return jnp.take(values, keep, axis=values.ndim - 1)


def spread_axis(values, which):
    lead = lax.slice_in_dim(values, 0, GCUT + 1, axis=which)
    tail = lax.slice_in_dim(values, GCUT + 1, 2 * GCUT + 1, axis=which)
    shape = list(values.shape)
    shape[which] = BOX - 2 * GCUT - 1
    return jnp.concatenate([lead, jnp.zeros(shape, values.dtype), tail], axis=which)


def box_of(values):
    for which in (values.ndim - 3, values.ndim - 2, values.ndim - 1):
        values = spread_axis(values, which)
    return values


def reference(psi_occ, energies, k_point, g_mask, v_local, dv):
    sphere = g_mask.reshape(BOX, BOX, BOX).astype(jnp.float32)
    occupied = complex_form(psi_occ.astype(jnp.float32)) * sphere
    occupied_cube = cube_of(occupied)
    solved = occupied[::STRIDE]
    freq = signed_freq()
    factor = 0.5 * (2.0 * math.pi / cell_length) ** 2
    kinetic = factor * ((freq[:, None, None] + k_point[0]) ** 2 + (freq[None, :, None] + k_point[1]) ** 2 + (freq[None, None, :] + k_point[2]) ** 2)
    potential = v_local.reshape(BOX, BOX, BOX)
    changes = dv.reshape(NPERT, BOX, BOX, BOX)
    grid_axes = (-3, -2, -1)

    def grid_apply(field, coeffs):
        real_space = jnp.fft.ifftn(coeffs, axes=grid_axes)
        return sphere * jnp.fft.fftn(field * real_space, axes=grid_axes)

    def project(values):
        part = cube_of(values)
        lowered = rounded(jnp.real(part)) + 1j * rounded(jnp.imag(part))
        correlation = jnp.einsum('mabc,sabc->ms', jnp.conj(occupied_cube), lowered, precision=lax.Precision.HIGHEST)
        low_correlation = rounded(jnp.real(correlation)) + 1j * rounded(jnp.imag(correlation))
        result = jnp.einsum('ms,mabc->sabc', low_correlation, occupied_cube, precision=lax.Precision.HIGHEST)
        return box_of(result) / BOX ** 3

    source = grid_apply(changes[None], solved[:, None]).reshape(NSOLVE * NPERT, BOX, BOX, BOX)
    right_side = project(source) - source
    shift = jnp.repeat(energies, NPERT)[:, None, None, None]

    def apply_operator(values):
        return (kinetic - shift) * values + grid_apply(potential, values) + shift_weight * project(values)

    def inner(first, second):
        total = jnp.real(first) * jnp.real(second) + jnp.imag(first) * jnp.imag(second)
        return jnp.sum(total, axis=(1, 2, 3)) / BOX ** 3

    response = jnp.zeros_like(right_side)
    residual = right_side
    direction = right_side
    norm_now = inner(residual, residual)
    for iteration in range(ITERS):
        image = apply_operator(direction)
        step_size = (norm_now / inner(direction, image))[:, None, None, None]
        response = response + step_size * direction
        residual = residual - step_size * image
        fresh = inner(residual, residual)
        direction = residual + (fresh / norm_now)[:, None, None, None] * direction
        norm_now = fresh

    def halves(values):
        joined = jnp.concatenate([jnp.real(values), jnp.imag(values)], axis=-1)
        return joined.reshape(NSOLVE, NPERT, BOX, BOX, 2 * BOX).astype(jnp.float32)

    return halves(response), halves(residual)
```

```python
import math

import jax
import jax.numpy as jnp
import numpy as np
from jax import lax
from jax.experimental import pallas as pl
from jax.experimental.pallas import tpu as pltpu
from jax.sharding import PartitionSpec as P

BOX = 64
GCUT = 21
KEPT = 2 * GCUT + 1
PADDED = 48
NPERT = 3
ITERS = 2
STRIDE = 16
MIDDLE = 2.5


cell_length = 16.5
shift_weight = 8.0


def quarter_turn(values):
    halfway = values.shape[-1] // 2
    return jnp.concatenate([-values[..., halfway:], values[..., :halfway]], axis=-1)


def minus_turn(values):
    halfway = values.shape[-1] // 2
    return jnp.concatenate([values[..., halfway:], -values[..., :halfway]], axis=-1)


def phase_tables(phase_sign):
    indices = np.arange(BOX)
    angle = (indices[:, None] * indices[None, :] % BOX) * (2.0 * math.pi / BOX)
    return np.cos(angle), phase_sign * np.sin(angle)


def kept_positions():
    return np.concatenate([np.arange(GCUT + 1), np.arange(BOX - GCUT, BOX)])


def split_table(table):
    table = np.asarray(table, np.float32)
    high = table.astype(jnp.bfloat16)
    low = (table - high.astype(np.float32)).astype(jnp.bfloat16)
    return np.stack([high, low])


def transform_tables():
    keep = kept_positions()
    tables = []
    for sign in (1.0, -1.0):
        cosine, sine = phase_tables(sign)
        lanes = np.block([[cosine, sine], [-sine, cosine]])
        first = np.concatenate([cosine, sine], axis=1)
        if sign > 0:
            second = np.zeros((BOX, 2 * PADDED))
            second[:, :KEPT] = cosine[:, keep]
            second[:, PADDED : PADDED + KEPT] = sine[:, keep]
        else:
            second = np.zeros((PADDED, 2 * BOX))
            second[:KEPT, :BOX] = cosine[keep]
            second[:KEPT, BOX:] = sine[keep]
        tables += [split_table(lanes), split_table(first), split_table(second)]
    return tables


def keep_rows(values, axis):
    lead = lax.slice_in_dim(values, 0, GCUT + 1, axis=axis)
    tail = lax.slice_in_dim(values, BOX - GCUT, BOX, axis=axis)
    return jnp.concatenate([lead, tail], axis=axis)


def grid_kernel(exact, x_ref, w_ref, li_ref, fi_ref, si_ref, lf_ref, ff_ref, sf_ref, o_ref, u_ref, t_ref, r_ref, q_ref):
    lane = lax.broadcasted_iota(jnp.int32, (1, 2 * BOX), 1)
    sign = jnp.where(lane < BOX, -1.0, 1.0).astype(jnp.float32)

    def plain(left, right):
        return jnp.dot(left, right, preferred_element_type=jnp.float32)

    def halves(values):
        high = values.astype(jnp.bfloat16)
        if not exact:
            return high, None
        return high, (values - high.astype(jnp.float32)).astype(jnp.bfloat16)

    def from_left(table_ref, values):
        turned = pltpu.roll(values, BOX, 1) * sign
        high, low = halves(jnp.concatenate([values, turned], axis=0))
        total = plain(table_ref[0], high)
        if exact:
            total = total + (plain(table_ref[1], high) + plain(table_ref[0], low))
        return total

    def from_right(values, table_ref):
        high, low = halves(values)
        total = plain(high, table_ref[0])
        if exact:
            total = total + (plain(high, table_ref[1]) + plain(low, table_ref[0]))
        return total

    @pl.when(pl.program_id(1) == 0)
    def _():
        t_ref[KEPT:] = jnp.zeros((PADDED - KEPT, BOX, 2 * BOX), jnp.float32)
        rows = x_ref[0].reshape(KEPT * BOX, 2 * BOX).astype(jnp.float32)
        u_ref[...] = from_right(rows, li_ref).reshape(KEPT, BOX, 2 * BOX)
        for b in range(KEPT):
            t_ref[b] = from_left(fi_ref, u_ref[b])
        for a in range(BOX):
            r_ref[a] = from_left(si_ref, t_ref[:, a, :])

    for a in range(BOX):
        q_ref[a] = from_left(sf_ref, r_ref[a] * w_ref[0, a])
    q_ref[...] = from_right(q_ref[...].reshape(BOX * PADDED, 2 * BOX), lf_ref).reshape(BOX, PADDED, 2 * BOX)
    for b in range(KEPT):
        o_ref[0, b] = from_left(ff_ref, q_ref[:, b, :]).astype(o_ref.dtype)


def apply_fields(coeffs, fields, tables, exact, out_type):
    count, spread = coeffs.shape[0], fields.shape[0]
    whole = lambda array: pl.BlockSpec(array.shape, lambda i, j: (0,) * array.ndim)
    return pl.pallas_call(
        lambda *refs: grid_kernel(exact, *refs),
        grid=(count, spread),
        in_specs=[
            pl.BlockSpec((1, KEPT, BOX, 2 * BOX), lambda i, j: (i, 0, 0, 0)),
            pl.BlockSpec((1, BOX, BOX, 2 * BOX), lambda i, j: (j, 0, 0, 0)),
        ]
        + [whole(table) for table in tables],
        out_specs=pl.BlockSpec((1, KEPT, BOX, 2 * BOX), lambda i, j: (i * spread + j, 0, 0, 0)),
        out_shape=jax.ShapeDtypeStruct((count * spread, KEPT, BOX, 2 * BOX), out_type),
        scratch_shapes=[
            pltpu.VMEM((KEPT, BOX, 2 * BOX), jnp.float32),
            pltpu.VMEM((PADDED, BOX, 2 * BOX), jnp.float32),
            pltpu.VMEM((BOX, BOX, 2 * BOX), jnp.float32),
            pltpu.VMEM((BOX, PADDED, 2 * BOX), jnp.float32),
        ],
        compiler_params=pltpu.CompilerParams(
            dimension_semantics=("arbitrary", "arbitrary"), vmem_limit_bytes=50 * 2**20
        ),
        name="grid_exact" if exact else "grid_apply",
    )(coeffs, fields, *tables)


def on_device(psi_occ, energies, k_point, g_mask, v_local, dv):
    slab_rows = psi_occ.shape[1]
    row_count = v_local.shape[1] // BOX
    ga_index = lax.axis_index("ga")
    signed = np.where(np.arange(BOX) < BOX // 2, np.arange(BOX), np.arange(BOX) - BOX).astype(np.float32)
    second_freq = jnp.asarray(signed[kept_positions()])
    signed = jnp.asarray(signed)
    owned = ga_index * slab_rows + jnp.arange(slab_rows, dtype=jnp.int32)
    freq_first = jnp.where(owned < BOX // 2, owned, owned - BOX).astype(jnp.float32)
    factor = 0.5 * (2.0 * math.pi / cell_length) ** 2
    kinetic = factor * (
        (freq_first[None, :, None] + k_point[0]) ** 2
        + (second_freq[:, None, None] + k_point[1]) ** 2
        + (signed[None, None, :] + k_point[2]) ** 2
    )
    kinetic = jnp.concatenate([kinetic, kinetic], axis=-1)
    sphere = keep_rows(g_mask.reshape(slab_rows, BOX, BOX), 1).transpose(1, 0, 2).astype(jnp.float32)
    sphere = jnp.concatenate([sphere, sphere], axis=-1)
    tables = [jnp.asarray(table) for table in transform_tables()]

    local_bands = energies.shape[0]

    def to_boxes(values):
        short = -values.shape[0] % lax.axis_size("ga")
        if short:
            values = jnp.concatenate([values, jnp.zeros((short,) + values.shape[1:], values.dtype)], axis=0)
        return lax.all_to_all(values, "ga", split_axis=0, concat_axis=2, tiled=True)

    low_sphere = sphere.astype(jnp.bfloat16)
    solved = keep_rows(psi_occ[::STRIDE], 2).transpose(0, 2, 1, 3) * low_sphere
    moved_solved = to_boxes(solved)

    fields = jnp.concatenate([dv, v_local[None] - MIDDLE], axis=0) / BOX**3
    fields = lax.all_gather(fields, "ga", axis=0)
    fields = fields.reshape(-1, NPERT + 1, BOX, row_count, BOX).transpose(1, 2, 0, 3, 4)
    fields = fields.reshape(NPERT + 1, BOX, BOX, BOX)
    fields = jnp.concatenate([fields, fields], axis=-1)
    changes, potential = fields[:NPERT], fields[NPERT:]

    occupied = keep_rows(psi_occ, 2).transpose(0, 2, 1, 3) * low_sphere
    flat_panel = lax.all_gather(
        occupied.reshape(occupied.shape[0], -1), "band", axis=0, tiled=True
    )
    energy_shift = jnp.repeat(energies, NPERT)[:, None, None, None]

    def project_occupied(values):
        count = values.shape[0]
        lowered = values.astype(jnp.bfloat16)
        stacked = jnp.concatenate([lowered, minus_turn(lowered)], axis=0).reshape(2 * count, -1)
        partial_value = lax.dot_general(
            flat_panel, stacked, (((1,), (1,)), ((), ())), preferred_element_type=jnp.float32
        )
        correlation = lax.psum(partial_value, "ga")
        low_correlation = correlation.astype(jnp.bfloat16)
        product = lax.dot_general(
            low_correlation,
            flat_panel,
            (((0,), (0,)), ((), ())),
            preferred_element_type=jnp.float32,
        )
        product = product.reshape(2 * count, KEPT, slab_rows, 2 * BOX)
        return (product[:count] + quarter_turn(product[count:])) / BOX**3

    def back_to_slabs(values):
        slabs = lax.all_to_all(values, "ga", split_axis=2, concat_axis=0, tiled=True)
        return slabs[: local_bands * NPERT].astype(jnp.float32) * sphere

    def local_inner(first, second):
        return jnp.sum(first * second, axis=(1, 2, 3)) / BOX**3

    diagonal = kinetic + MIDDLE - energy_shift

    def operator(direction):
        moved = to_boxes(direction.astype(jnp.bfloat16))
        applied = back_to_slabs(apply_fields(moved, potential, tables, False, jnp.bfloat16))
        return diagonal * direction + applied + shift_weight * project_occupied(direction)

    source = back_to_slabs(apply_fields(moved_solved, changes, tables, True, jnp.float32))
    right_side = project_occupied(source) - source
    residual = right_side
    direction = right_side
    response = None
    norm_now = None
    for iteration in range(ITERS):
        image = operator(direction)
        sums = [local_inner(direction, image)]
        if iteration == 0:
            sums.append(local_inner(residual, residual))
        if iteration + 1 < ITERS:
            sums += [local_inner(residual, image), local_inner(image, image)]
        sums = lax.psum(jnp.stack(sums), "ga")
        if iteration == 0:
            norm_now = sums[1]
        step_size = norm_now / sums[0]
        step = step_size[:, None, None, None]
        response = step * direction if response is None else response + step * direction
        residual = residual - step * image
        if iteration + 1 < ITERS:
            fresh = norm_now - 2.0 * step_size * sums[-2] + step_size**2 * sums[-1]
            direction = residual + (fresh / norm_now)[:, None, None, None] * direction
            norm_now = fresh

    def restore(values):
        values = values.transpose(0, 2, 1, 3)
        filler = jnp.zeros(values.shape[:2] + (BOX - KEPT, 2 * BOX), values.dtype)
        values = jnp.concatenate([values[:, :, : GCUT + 1], filler, values[:, :, GCUT + 1 :]], axis=2)
        return values.reshape(local_bands, NPERT, slab_rows, BOX, 2 * BOX)

    return (restore(response), restore(residual))


def solution(mesh):
    placed = (
        P(("pool", "band"), "ga", None, None),
        P(("pool", "band")),
        P("pool"),
        P(("pool", "ga"), None),
        P(None, "ga"),
        P(None, None, "ga"),
    )
    return jax.shard_map(
        on_device,
        mesh=mesh,
        in_specs=placed,
        out_specs=(
            P(("pool", "band"), None, "ga", None, None),
            P(("pool", "band"), None, "ga", None, None),
        ),
        check_vma=False,
    )
```
